512 devices in a mesh: prow: 16 (over y, core), pcol: 32 (over z, x).
Axes of the slice: x: 4, y: 8, z: 8, core: 2. Of those that a mesh axis runs over, the one named last changes fastest.
Arguments:
- stiffness: float32 [4, 16, 2, 32, 256, 256], P(None, 'prow', None, 'pcol'), may hold values from -1 to 33, as said below
- pattern: int32 [2, 64], replicated, may hold values 0 or 1
Outputs:
- factored: float32 [4, 16, 2, 32, 256, 256], P(None, 'prow', None, 'pcol')
The draws below stay inside these ranges and needn't reach their ends.
Inputs may be any that keep to these rules, and one draw needn't show every extreme that they name: `stiffness`: Symmetric; entries off the main diagonal have magnitude at most 1, and the main diagonal's entries lie between 31 and 33.
All inputs are finite; a program needn't handle non-finite values.
Results may differ from the reference program's by a relative error of at most 0.0003.
Values sent between devices are 32-bit elements; how exact they have to be, the bound alone decides.
A program may use at most 64 MiB of HBM per device.

```python
import jax
import jax.numpy as jnp
from jax import lax

B = 256
BR_DEV = 4
NB = 64
N_PROW = 16
N_PCOL = 32


def draw_stiffness(key, part):
    count = BR_DEV * N_PROW
    entries = jax.random.uniform(key, (count, count, B, B), jnp.float32, -1.0, 1.0)
    symmetric = 0.5 * (entries + jnp.transpose(entries, (1, 0, 3, 2)))
    same_block = (jnp.arange(count)[:, None] == jnp.arange(count)[None, :]).astype(jnp.float32)
    same_entry = jnp.eye(B, dtype=jnp.float32)
    diagonal_add = 32.0 * same_block[:, :, None, None] * same_entry[None, None, :, :]
    return (symmetric + diagonal_add).reshape(BR_DEV, N_PROW, count // N_PCOL, N_PCOL, B, B)


def plant(values, key, low, top_value):
    longest = values.shape.index(max(values.shape))
    spots = []
    for shift in (0, 1):
        where = [jax.random.randint(jax.random.fold_in(key, axis), (), 0, length) for axis, length in enumerate(values.shape)]
        where[longest] = (where[longest] + shift) % values.shape[longest]
        spots.append(tuple(where))
    return values.at[spots[0]].set(low).at[spots[1]].set(top_value)


def setup_inputs(seed: int = 0) -> dict:
    key_list = jax.random.split(jax.random.key(seed), 3)
    return {
        "stiffness": draw_stiffness(jax.random.fold_in(key_list[2], 71), 0),
        "pattern": plant((jax.random.randint(key_list[1], (2, NB), 0, 4) < 3).astype(jnp.int32), jax.random.fold_in(key_list[1], 1), 0, 1),
    }


def solve_blocks(factor, blocks):
    count = blocks.shape[0]
    right_hand = jnp.transpose(blocks, (2, 0, 1)).reshape(B, count * B)
    solved = lax.linalg.triangular_solve(factor, right_hand, left_side=True, lower=True)
    return jnp.transpose(solved.reshape(B, count, B), (1, 2, 0))

def reference(stiffness, pattern):
    matrix = stiffness.reshape(NB, NB, B, B)
    block_index = jnp.arange(NB, dtype=jnp.int32)
    first_flags = (pattern[0] == 1) & (block_index > 0)
    second_flags = ((pattern[1] == 1) | first_flags[1] & first_flags) & (block_index > 1)
    for column, flags in ((0, first_flags), (1, second_flags)):
        factor = jnp.linalg.cholesky(matrix[column, column])
        solved = solve_blocks(factor, matrix[:, column])
        panel_blocks = jnp.where(flags[:, None, None], solved, jnp.zeros_like(solved))

        def one_row(row):
            product = jnp.einsum('ab,jcb->jac', panel_blocks[row], panel_blocks, precision=lax.Precision.HIGHEST)
            keep_mask = (block_index > column) & (block_index <= row)
            return matrix[row] - jnp.where(keep_mask[:, None, None], product, jnp.zeros_like(product))
        updated = lax.map(one_row, block_index)
        below = (block_index > column)[:, None, None]
        new_column = jnp.where(below, panel_blocks, matrix[:, column])
        new_column = new_column.at[column].set(factor)
        matrix = updated.at[:, column].set(new_column)
    return matrix.reshape(stiffness.shape)
```

```python
import jax
import jax.numpy as jnp
from jax import lax
from jax.experimental import pallas as pl
from jax.experimental.pallas import tpu as pltpu
from jax.sharding import PartitionSpec as P

B = 256
PANEL = 32
SUB = 8
LANES = 128
WINDOW = 3 * LANES
F32 = jnp.float32
BF16 = jnp.bfloat16


def split(x):
    high = x.astype(BF16)
    return high, (x - high.astype(F32)).astype(BF16)


def product(a, b, dims):
    dot = lambda x, y: lax.dot_general(x, y, (dims, ((), ())), preferred_element_type=F32)
    return dot(a[0], b[0]) + (dot(a[0], b[1]) + dot(a[1], b[0]))


NT = ((1,), (1,))
NN = ((1,), (0,))


def eliminate(work):
    spread = lambda x: jnp.broadcast_to(x, (SUB, LANES))
    sublane = lax.broadcasted_iota(jnp.int32, (SUB, WINDOW), 0)
    for top in range(0, B, PANEL):
        off = top // LANES * LANES
        groups = [work[top + SUB * q:top + SUB * (q + 1), off:off + WINDOW] for q in range(PANEL // SUB)]
        for g in range(PANEL // SUB):
            lane = top + SUB * g - off
            columns = [
                [spread(groups[q][:, lane + j:lane + j + 1]) for j in range(SUB)]
                for q in range(g, PANEL // SUB)
            ]
            s = [[spread(columns[0][j][i:i + 1, :]) for j in range(i + 1)] for i in range(SUB)]
            inverse = []
            for j in range(SUB):
                inverse.append(lax.rsqrt(s[j][j]))
                for i in range(j + 1, SUB):
                    s[i][j] = s[i][j] * inverse[j]
                for k in range(j + 1, SUB):
                    for i in range(k, SUB):
                        s[i][k] = s[i][k] - s[i][j] * s[k][j]
            wide = lambda x: jnp.concatenate([x] * (WINDOW // LANES), axis=1)
            rows = []
            result = None
            for j in range(SUB):
                row = jnp.broadcast_to(groups[g][j:j + 1, :], (SUB, WINDOW))
                for m in range(j):
                    row = row - wide(s[j][m]) * rows[m]
                row = row * wide(inverse[j])
                rows.append(row)
                result = row if result is None else jnp.where(sublane == j, row, result)
            groups[g] = result
            for q in range(g + 1, PANEL // SUB):
                cols = []
                total = groups[q]
                for j in range(SUB):
                    col = columns[q - g][j]
                    for m in range(j):
                        col = col - cols[m] * s[j][m]
                    col = col * inverse[j]
                    cols.append(col)
                    total = total - wide(col) * rows[j]
                groups[q] = total
        panel = jnp.concatenate(groups, axis=0)
        work[top:top + PANEL, off:off + WINDOW] = panel
        rest = top + PANEL
        if rest < B:
            start = rest // LANES * LANES
            left = split(panel[:, start - off:B - off].T)
            update = product(left, split(panel), NN)[rest - start:]
            work[rest:, off:off + WINDOW] = work[rest:, off:off + WINDOW] - update


def finish(work, factor_ref, inverse_ref):
    row = lax.broadcasted_iota(jnp.int32, (B, B), 0)
    col = lax.broadcasted_iota(jnp.int32, (B, B), 1)
    factor_ref[...] = jnp.where(col >= row, work[:, :B], 0.0).T
    inverse_ref[...] = work[:, B:]


def start(work, block):
    row = lax.broadcasted_iota(jnp.int32, (B, B), 0)
    col = lax.broadcasted_iota(jnp.int32, (B, B), 1)
    work[:, :B] = block
    work[:, B:] = jnp.where(row == col, 1.0, 0.0).astype(F32)


def first_kernel(block_ref, factor_ref, inverse_ref, work):
    start(work, block_ref[...])
    eliminate(work)
    finish(work, factor_ref, inverse_ref)


def second_kernel(flag_ref, pair_ref, w_ref, lower_ref, factor_ref, inverse_ref, work):
    lower = product(split(pair_ref[0]), split(w_ref[...]), NT)
    lower = jnp.where(flag_ref[0] > 0, lower, jnp.zeros_like(lower))
    lower_ref[...] = lower
    parts = split(lower)
    start(work, pair_ref[1] - product(parts, parts, NT))
    eliminate(work)
    finish(work, factor_ref, inverse_ref)


SQUARE = jax.ShapeDtypeStruct((B, B), F32)
ELIMINATION = pl.CostEstimate(flops=2 * B * B * B, bytes_accessed=24 << 20, transcendentals=0)


def factor_first(block):
    return pl.pallas_call(
        first_kernel,
        out_shape=(SQUARE, SQUARE),
        scratch_shapes=[pltpu.VMEM((B, 2 * B), F32)],
        cost_estimate=ELIMINATION,
        name="factor_first",
    )(block)


def factor_second(flag, pair, w):
    vmem = pl.BlockSpec(memory_space=pltpu.VMEM)
    return pl.pallas_call(
        second_kernel,
        out_shape=(SQUARE, SQUARE, SQUARE),
        in_specs=[pl.BlockSpec(memory_space=pltpu.SMEM), vmem, vmem],
        scratch_shapes=[pltpu.VMEM((B, 2 * B), F32)],
        cost_estimate=ELIMINATION,
        name="factor_second",
    )(flag, pair, w)


def panel_rows(first, second, flag0, flag1, w0, w1, lower):
    l0 = product(split(first), w0, NT)
    l0 = jnp.where(flag0, l0, jnp.zeros_like(l0))
    p0 = split(l0)
    l1 = product(split(second - product(p0, lower, NT)), w1, NT)
    l1 = jnp.where(flag1, l1, jnp.zeros_like(l1))
    return l0, l1, p0, split(l1)


def trailing_kernel(
    info, blocks_ref, rows_ref, cols_ref, w0_ref, w1_ref, lower_ref, g0_ref, g1_ref, out_ref,
    high0, low0, high1, low1, weights
):
    a = pl.program_id(0)
    count_c = high0.shape[0]
    count_r = pl.num_programs(0)

    @pl.when(a == 0)
    def _():
        for n, ref in enumerate((w0_ref, w1_ref, lower_ref)):
            weights[2 * n], weights[2 * n + 1] = split(ref[...])
        for b in range(count_c):
            flags = info[2 + 2 * count_r + b], info[2 + 2 * count_r + count_c + b]
            w0, w1, lower = ((weights[2 * n], weights[2 * n + 1]) for n in range(3))
            _, _, p0, p1 = panel_rows(
                cols_ref[0, b], cols_ref[1, b], flags[0] > 0, flags[1] > 0, w0, w1, lower
            )
            high0[b], low0[b] = p0
            high1[b], low1[b] = p1

    w0, w1, lower = ((weights[2 * n], weights[2 * n + 1]) for n in range(3))
    l0, l1, p0, p1 = panel_rows(
        rows_ref[0, 0], rows_ref[1, 0], info[2 + a] > 0, info[2 + count_r + a] > 0, w0, w1, lower
    )
    row = info[0] + info[2 + 2 * count_r + 2 * count_c] * a
    for b in range(count_c):
        col = info[1] + info[3 + 2 * count_r + 2 * count_c] * b
        old = blocks_ref[0, b]

        @pl.when(col > row)
        def _():
            out_ref[0, b] = old

        @pl.when(col == 0)
        def _():
            out_ref[0, b] = jnp.where(row == 0, g0_ref[...], l0)

        @pl.when((col == 1) & (row >= 1))
        def _():
            out_ref[0, b] = jnp.where(row == 1, g1_ref[...], l1)

        @pl.when((col > 1) & (col <= row))
        def _():
            update = product(p0, (high0[b], low0[b]), NT) + product(p1, (high1[b], low1[b]), NT)
            out_ref[0, b] = old - update


def trailing(info, blocks, rows, cols, w0, w1, lower, g0, g1):
    count_r, count_c = blocks.shape[0], blocks.shape[1]
    whole = lambda shape: pl.BlockSpec(shape, lambda a: (0,) * len(shape))
    own = pl.BlockSpec((1, count_c, B, B), lambda a: (a, 0, 0, 0))
    return pl.pallas_call(
        trailing_kernel,
        grid=(count_r,),
        out_shape=jax.ShapeDtypeStruct(blocks.shape, F32),
        in_specs=[
            pl.BlockSpec(memory_space=pltpu.SMEM),
            own,
            pl.BlockSpec((2, 1, B, B), lambda a: (0, a, 0, 0)),
            whole((2, count_c, B, B)),
        ] + [whole((B, B))] * 5,
        out_specs=own,
        scratch_shapes=[pltpu.VMEM((count_c, B, B), BF16)] * 4 + [pltpu.VMEM((6, B, B), BF16)],
        name="trailing",
    )(info, blocks, rows, cols, w0, w1, lower, g0, g1)


def local(stiffness, pattern):
    row_count, col_count = stiffness.shape[0], stiffness.shape[2]
    nprow, npcol = lax.axis_size("prow"), lax.axis_size("pcol")
    my_row, my_col = lax.axis_index("prow"), lax.axis_index("pcol")
    blocks = stiffness.reshape(row_count, col_count, B, B)
    both = ("prow", "pcol")
    only = lambda here, x: jnp.where(here, x, jnp.zeros_like(x))

    corner = blocks[0, 0]
    block00 = lax.psum(only((my_row == 0) & (my_col == 0), corner), both)
    pair = lax.psum(
        jnp.stack([only((my_row == 1) & (my_col == n), corner) for n in (0, 1)]), both
    )
    block00, pair, leading = lax.optimization_barrier((block00, pair, blocks[:, 0]))
    rows = lax.psum(jnp.stack([only(my_col == n, leading) for n in (0, 1)]), "pcol")
    g0, w0 = factor_first(block00)
    w0, rows = lax.optimization_barrier((w0, rows))

    glob_rows = my_row + nprow * jnp.arange(row_count, dtype=jnp.int32)
    glob_cols = my_col + npcol * jnp.arange(col_count, dtype=jnp.int32)
    wanted = jnp.take(rows, glob_cols // nprow, axis=1)
    cols = lax.psum(only(my_row == my_col % nprow, wanted), "prow")

    all_rows = jnp.arange(row_count * nprow, dtype=jnp.int32)
    flags0 = (pattern[0] == 1) & (all_rows > 0)
    flags1 = ((pattern[1] == 1) | flags0[1] & flags0) & (all_rows > 1)
    info = jnp.concatenate([
        jnp.stack([my_row, my_col]),
        jnp.take(flags0, glob_rows), jnp.take(flags1, glob_rows),
        jnp.take(flags0, glob_cols), jnp.take(flags1, glob_cols),
        jnp.array([nprow, npcol]),
    ]).astype(jnp.int32)

    lower, g1, w1 = factor_second(flags0[1:2].astype(jnp.int32), pair, w0)
    return trailing(info, blocks, rows, cols, w0, w1, lower, g0, g1).reshape(stiffness.shape)


def solution(mesh):
    placed = P(None, "prow", None, "pcol", None, None)
    return jax.shard_map(
        local, mesh=mesh, in_specs=(placed, P()), out_specs=placed, check_vma=False
    )
```

```python
import jax
import jax.numpy as jnp
from jax import lax
from jax.experimental import pallas as pl
from jax.experimental.pallas import tpu as pltpu
from jax.sharding import PartitionSpec as P

B = 256
PANEL = 32
SUB = 8
LANES = 128
WINDOW = 3 * LANES
F32 = jnp.float32
BF16 = jnp.bfloat16


def split(x):
    high = x.astype(BF16)
    return high, (x - high.astype(F32)).astype(BF16)


def product(a, b, dims):
    dot = lambda x, y: lax.dot_general(x, y, (dims, ((), ())), preferred_element_type=F32)
    return dot(a[0], b[0]) + (dot(a[0], b[1]) + dot(a[1], b[0]))


NT = ((1,), (1,))
NN = ((1,), (0,))


def eliminate(work):
    spread = lambda x: jnp.broadcast_to(x, (SUB, LANES))
    sublane = lax.broadcasted_iota(jnp.int32, (SUB, WINDOW), 0)
    for top in range(0, B, PANEL):
        off = top // LANES * LANES
        groups = [work[top + SUB * q:top + SUB * (q + 1), off:off + WINDOW] for q in range(PANEL // SUB)]
        for g in range(PANEL // SUB):
            lane = top + SUB * g - off
            columns = [
                [spread(groups[q][:, lane + j:lane + j + 1]) for j in range(SUB)]
                for q in range(g, PANEL // SUB)
            ]
            s = [[spread(columns[0][j][i:i + 1, :]) for j in range(i + 1)] for i in range(SUB)]
            inverse = []
            for j in range(SUB):
                inverse.append(lax.rsqrt(s[j][j]))
                for i in range(j + 1, SUB):
                    s[i][j] = s[i][j] * inverse[j]
                for k in range(j + 1, SUB):
                    for i in range(k, SUB):
                        s[i][k] = s[i][k] - s[i][j] * s[k][j]
            wide = lambda x: jnp.concatenate([x] * (WINDOW // LANES), axis=1)
            rows = []
            result = None
            for j in range(SUB):
                row = jnp.broadcast_to(groups[g][j:j + 1, :], (SUB, WINDOW))
                for m in range(j):
                    row = row - wide(s[j][m]) * rows[m]
                row = row * wide(inverse[j])
                rows.append(row)
                result = row if result is None else jnp.where(sublane == j, row, result)
            groups[g] = result
            for q in range(g + 1, PANEL // SUB):
                cols = []
                total = groups[q]
                for j in range(SUB):
                    col = columns[q - g][j]
                    for m in range(j):
                        col = col - cols[m] * s[j][m]
                    col = col * inverse[j]
                    cols.append(col)
                    total = total - wide(col) * rows[j]
                groups[q] = total
        panel = jnp.concatenate(groups, axis=0)
        work[top:top + PANEL, off:off + WINDOW] = panel
        rest = top + PANEL
        if rest < B:
            start = rest // LANES * LANES
            left = split(panel[:, start - off:B - off].T)
            update = product(left, split(panel), NN)[rest - start:]
            work[rest:, off:off + WINDOW] = work[rest:, off:off + WINDOW] - update


def finish(work, factor_ref, inverse_ref):
    row = lax.broadcasted_iota(jnp.int32, (B, B), 0)
    col = lax.broadcasted_iota(jnp.int32, (B, B), 1)
    factor_ref[...] = jnp.where(col >= row, work[:, :B], 0.0).T
    inverse_ref[...] = work[:, B:]


def start(work, block):
    row = lax.broadcasted_iota(jnp.int32, (B, B), 0)
    col = lax.broadcasted_iota(jnp.int32, (B, B), 1)
    work[:, :B] = block
    work[:, B:] = jnp.where(row == col, 1.0, 0.0).astype(F32)


def first_kernel(block_ref, factor_ref, inverse_ref, work):
    start(work, block_ref[...])
    eliminate(work)
    finish(work, factor_ref, inverse_ref)


def second_kernel(flag_ref, pair_ref, w_ref, lower_ref, factor_ref, inverse_ref, work):
    lower = product(split(pair_ref[0]), split(w_ref[...]), NT)
    lower = jnp.where(flag_ref[0] > 0, lower, jnp.zeros_like(lower))
    lower_ref[...] = lower
    parts = split(lower)
    start(work, pair_ref[1] - product(parts, parts, NT))
    eliminate(work)
    finish(work, factor_ref, inverse_ref)


SQUARE = jax.ShapeDtypeStruct((B, B), F32)
ELIMINATION = pl.CostEstimate(flops=2 * B * B * B, bytes_accessed=24 << 20, transcendentals=0)


def factor_first(block):
    return pl.pallas_call(
        first_kernel,
        out_shape=(SQUARE, SQUARE),
        scratch_shapes=[pltpu.VMEM((B, 2 * B), F32)],
        cost_estimate=ELIMINATION,
        name="factor_first",
    )(block)


def factor_second(flag, pair, w):
    vmem = pl.BlockSpec(memory_space=pltpu.VMEM)
    return pl.pallas_call(
        second_kernel,
        out_shape=(SQUARE, SQUARE, SQUARE),
        in_specs=[pl.BlockSpec(memory_space=pltpu.SMEM), vmem, vmem],
        scratch_shapes=[pltpu.VMEM((B, 2 * B), F32)],
        cost_estimate=ELIMINATION,
        name="factor_second",
    )(flag, pair, w)


def panel_rows(first, second, flag0, flag1, w0, w1, lower):
    l0 = product(split(first), w0, NT)
    l0 = jnp.where(flag0, l0, jnp.zeros_like(l0))
    p0 = split(l0)
    l1 = product(split(second - product(p0, lower, NT)), w1, NT)
    l1 = jnp.where(flag1, l1, jnp.zeros_like(l1))
    return l0, l1, p0, split(l1)


def trailing_kernel(
    info, blocks_ref, rows_ref, cols_ref, w0_ref, w1_ref, lower_ref, g0_ref, g1_ref, out_ref,
    high0, low0, high1, low1, weights
):
    a = pl.program_id(0)
    count_c = high0.shape[0]
    count_r = pl.num_programs(0)

    @pl.when(a == 0)
    def _():
        for n, ref in enumerate((w0_ref, w1_ref, lower_ref)):
            weights[2 * n], weights[2 * n + 1] = split(ref[...])
        for b in range(count_c):
            flags = info[2 + 2 * count_r + b], info[2 + 2 * count_r + count_c + b]
            w0, w1, lower = ((weights[2 * n], weights[2 * n + 1]) for n in range(3))
            _, _, p0, p1 = panel_rows(
                cols_ref[0, b], cols_ref[1, b], flags[0] > 0, flags[1] > 0, w0, w1, lower
            )
            high0[b], low0[b] = p0
            high1[b], low1[b] = p1

    w0, w1, lower = ((weights[2 * n], weights[2 * n + 1]) for n in range(3))
    l0, l1, p0, p1 = panel_rows(
        rows_ref[0, 0], rows_ref[1, 0], info[2 + a] > 0, info[2 + count_r + a] > 0, w0, w1, lower
    )
    row = info[0] + info[2 + 2 * count_r + 2 * count_c] * a
    for b in range(count_c):
        col = info[1] + info[3 + 2 * count_r + 2 * count_c] * b
        old = blocks_ref[0, b]

        @pl.when(col > row)
        def _():
            out_ref[0, b] = old

        @pl.when(col == 0)
        def _():
            out_ref[0, b] = jnp.where(row == 0, g0_ref[...], l0)

        @pl.when((col == 1) & (row >= 1))
        def _():
            out_ref[0, b] = jnp.where(row == 1, g1_ref[...], l1)

        @pl.when((col > 1) & (col <= row))
        def _():
            update = product(p0, (high0[b], low0[b]), NT) + product(p1, (high1[b], low1[b]), NT)
            out_ref[0, b] = old - update


def trailing(info, blocks, rows, cols, w0, w1, lower, g0, g1):
    count_r, count_c = blocks.shape[0], blocks.shape[1]
    whole = lambda shape: pl.BlockSpec(shape, lambda a: (0,) * len(shape))
    own = pl.BlockSpec((1, count_c, B, B), lambda a: (a, 0, 0, 0))
    return pl.pallas_call(
        trailing_kernel,
        grid=(count_r,),
        out_shape=jax.ShapeDtypeStruct(blocks.shape, F32),
        in_specs=[
            pl.BlockSpec(memory_space=pltpu.SMEM),
            own,
            pl.BlockSpec((2, 1, B, B), lambda a: (0, a, 0, 0)),
            whole((2, count_c, B, B)),
        ] + [whole((B, B))] * 5,
        out_specs=own,
        scratch_shapes=[pltpu.VMEM((count_c, B, B), BF16)] * 4 + [pltpu.VMEM((6, B, B), BF16)],
        name="trailing",
    )(info, blocks, rows, cols, w0, w1, lower, g0, g1)


CHIPS_X, CHIPS_Y, CHIPS_Z = 4, 8, 8
PIECES = 8
MESH = pl.DeviceIdType.MESH


def spread_kernel(
    lead, rows, cols, corner, x_send, x_recv, z_send, z_recv, y_send, y_recv, core_send, core_recv, here
):
    prow, pcol = lax.axis_index("prow"), lax.axis_index("pcol")
    y, core = prow // 2, prow % 2
    z, x = pcol // CHIPS_X, pcol % CHIPS_X
    order = lead.shape[1]
    piece = order * 4 // (2 * PIECES)

    def at_x(step):
        return {"pcol": z * CHIPS_X + (x + step + CHIPS_X) % CHIPS_X}

    def at_z(step):
        return {"pcol": (z + step + CHIPS_Z) % CHIPS_Z * CHIPS_X + x}

    def at_y(step):
        return {"prow": (y + step + CHIPS_Y) % CHIPS_Y * 2 + core}

    partner = {"prow": y * 2 + 1 - core}
    neighbours = [at(step) for at in (at_x, at_z, at_y) for step in (1, -1)] + [partner]
    barrier = pltpu.get_barrier_semaphore()
    for device in neighbours:
        pl.semaphore_signal(barrier, inc=1, device_id=device, device_id_type=MESH)
    pl.semaphore_wait(barrier, len(neighbours))

    def remote(ref, send, recv, device):
        return pltpu.make_async_remote_copy(
            src_ref=ref, dst_ref=ref, send_sem=send, recv_sem=recv, device_id=device, device_id_type=MESH
        )

    for n in (0, 1):
        @pl.when(pcol == n)
        def _():
            copy = pltpu.make_async_copy(lead, rows.at[n], here)
            copy.start()
            copy.wait()

    streams = []
    for n in (0, 1):
        for h in (0, 1):
            in_x = (x + CHIPS_X - n) % CHIPS_X if h == 0 else (n + CHIPS_X - x) % CHIPS_X
            in_z = z if h == 0 else (CHIPS_Z - z) % CHIPS_Z
            streams.append((n, h, in_x, in_z))
    deepest = streams[0][2] + streams[0][3]
    for _, _, in_x, in_z in streams[1:]:
        deepest = jnp.maximum(deepest, in_x + in_z)

    def row_copies(n, h, p):
        per = 2 * piece * (PIECES // 4) // 2
        first = pl.multiple_of(h * per + p % (PIECES // 4) * piece, piece)
        ref = rows.at[n, p // (PIECES // 4), pl.ds(first, piece)]
        k = (n * 2 + h) * PIECES + p
        step = 1 if h == 0 else -1
        return (
            remote(ref, x_send.at[k], x_recv.at[k], at_x(step)),
            remote(ref, z_send.at[k], z_recv.at[k], at_z(step)),
        )

    half_order = order // 2
    items = []
    for q in range(3):
        for k in (0, 1):
            part = pl.ds(k * half_order, half_order)
            source = min(q, 1)
            items.append((deepest + 2 + 2 * q + k, source, rows.at[q // 2, 0, part], corner.at[q, part]))
    wanted = pcol // (2 * CHIPS_Y)
    for b in (0, 1):
        for n in (0, 1):
            for k in (0, 1):
                part = pl.ds(k * half_order, half_order)
                when = deepest + (PIECES // 2 + 2 if b == 0 else PIECES) + 2 * n + k
                items.append(
                    (when, pcol % (2 * CHIPS_Y), rows.at[n, wanted + 2 * b, part], cols.at[n, b, part])
                )
    far = CHIPS_Y // 2

    def item_copies(k, ref):
        return (
            remote(ref, y_send.at[2 * k], y_recv.at[k], at_y(1)),
            remote(ref, y_send.at[2 * k + 1], y_recv.at[k], at_y(-1)),
            remote(ref, core_send.at[k], core_recv.at[k], partner),
        )

    def place(source):
        ahead = (y + CHIPS_Y - source // 2) % CHIPS_Y
        up = ahead < far
        down = (ahead == 0) | (ahead > far + 1) if CHIPS_Y > 2 else ahead < 0
        return ahead, jnp.minimum(ahead, CHIPS_Y - ahead), up, down

    def step(t, carry):
        for n, h, in_x, in_z in streams:
            p = t - in_x - in_z

            @pl.when((p >= 0) & (p < PIECES))
            def _():
                along_x, along_z = row_copies(n, h, p)

                @pl.when((in_z == 0) & (in_x > 0))
                def _():
                    along_x.wait_recv()

                @pl.when(in_z > 0)
                def _():
                    along_z.wait_recv()

                @pl.when((in_z == 0) & (in_x < CHIPS_X - 1))
                def _():
                    along_x.start()

                @pl.when(in_z < CHIPS_Z - 1)
                def _():
                    along_z.start()

        for k, (when, source, origin, ref) in enumerate(items):
            ahead, depth, up, down = place(source)
            above, below, across = item_copies(k, ref)

            @pl.when((t == when + depth) & (core == source % 2))
            def _():
                @pl.when(ahead == 0)
                def _():
                    copy = pltpu.make_async_copy(origin, ref, here)
                    copy.start()
                    copy.wait()

                @pl.when(ahead > 0)
                def _():
                    above.wait_recv()

                @pl.when(up)
                def _():
                    above.start()

                @pl.when(down)
                def _():
                    below.start()

                across.start()

            @pl.when((t == when + depth + 1) & (core != source % 2))
            def _():
                across.wait_recv()

        return carry

    steps = CHIPS_X + CHIPS_Z - 2 + PIECES + 4 + far + 2
    lax.fori_loop(0, steps, step, 0)

    def drain(p, carry):
        for n, h, in_x, in_z in streams:
            along_x, along_z = row_copies(n, h, p)

            @pl.when((in_z == 0) & (in_x < CHIPS_X - 1))
            def _():
                along_x.wait_send()

            @pl.when(in_z < CHIPS_Z - 1)
            def _():
                along_z.wait_send()

        return carry

    lax.fori_loop(0, PIECES, drain, 0)
    for k, (_, source, _, ref) in enumerate(items):
        _, _, up, down = place(source)
        above, below, across = item_copies(k, ref)

        @pl.when(core == source % 2)
        def _():
            @pl.when(up)
            def _():
                above.wait_send()

            @pl.when(down)
            def _():
                below.wait_send()

            across.wait_send()


def spread(lead):
    count, order = lead.shape[0], lead.shape[1]
    vmem = pl.BlockSpec(memory_space=pltpu.VMEM)
    shapes = ((2, count, order, order), (2, 2, order, order), (3, order, order))
    dma = pltpu.SemaphoreType.DMA
    return pl.pallas_call(
        spread_kernel,
        out_shape=tuple(jax.ShapeDtypeStruct(shape, F32) for shape in shapes),
        in_specs=[vmem],
        out_specs=(vmem,) * 3,
        scratch_shapes=[dma((4 * PIECES,))] * 4 + [dma((28,)), dma((14,)), dma((14,)), dma((14,)), dma(())],
        compiler_params=pltpu.CompilerParams(collective_id=0, has_side_effects=True),
        name="spread",
    )(lead)


def local(stiffness, pattern):
    row_count, col_count = stiffness.shape[0], stiffness.shape[2]
    nprow, npcol = lax.axis_size("prow"), lax.axis_size("pcol")
    my_row, my_col = lax.axis_index("prow"), lax.axis_index("pcol")
    blocks = stiffness.reshape(row_count, col_count, B, B)
    rows, cols, corner = spread(blocks[:, 0])
    g0, w0 = factor_first(corner[0])
    glob_rows = my_row + nprow * jnp.arange(row_count, dtype=jnp.int32)
    glob_cols = my_col + npcol * jnp.arange(col_count, dtype=jnp.int32)
    all_rows = jnp.arange(row_count * nprow, dtype=jnp.int32)
    flags0 = (pattern[0] == 1) & (all_rows > 0)
    flags1 = ((pattern[1] == 1) | flags0[1] & flags0) & (all_rows > 1)
    info = jnp.concatenate([
        jnp.stack([my_row, my_col]),
        jnp.take(flags0, glob_rows), jnp.take(flags1, glob_rows),
        jnp.take(flags0, glob_cols), jnp.take(flags1, glob_cols),
        jnp.array([nprow, npcol]),
    ]).astype(jnp.int32)

    lower, g1, w1 = factor_second(flags0[1:2].astype(jnp.int32), corner[1:], w0)
    return trailing(info, blocks, rows, cols, w0, w1, lower, g0, g1).reshape(stiffness.shape)


def solution(mesh):
    placed = P(None, "prow", None, "pcol", None, None)
    return jax.shard_map(
        local, mesh=mesh, in_specs=(placed, P()), out_specs=placed, check_vma=False
    )
```

```python
import jax
import jax.numpy as jnp
from jax import lax
from jax.experimental import pallas as pl
from jax.experimental.pallas import tpu as pltpu
from jax.sharding import PartitionSpec as P

B = 256
PANEL = 32
SUB = 8
LANES = 128
WINDOW = 3 * LANES
F32 = jnp.float32
BF16 = jnp.bfloat16


def split(x):
    high = x.astype(BF16)
    return high, (x - high.astype(F32)).astype(BF16)


def product(a, b, dims):
    dot = lambda x, y: lax.dot_general(x, y, (dims, ((), ())), preferred_element_type=F32)
    return dot(a[0], b[0]) + (dot(a[0], b[1]) + dot(a[1], b[0]))


NT = ((1,), (1,))
NN = ((1,), (0,))


def eliminate(work):
    spread = lambda x: jnp.broadcast_to(x, (SUB, LANES))
    sublane = lax.broadcasted_iota(jnp.int32, (SUB, WINDOW), 0)
    for top in range(0, B, PANEL):
        off = top // LANES * LANES
        groups = [work[top + SUB * q:top + SUB * (q + 1), off:off + WINDOW] for q in range(PANEL // SUB)]
        for g in range(PANEL // SUB):
            lane = top + SUB * g - off
            columns = [
                [spread(groups[q][:, lane + j:lane + j + 1]) for j in range(SUB)]
                for q in range(g, PANEL // SUB)
            ]
            s = [[spread(columns[0][j][i:i + 1, :]) for j in range(i + 1)] for i in range(SUB)]
            inverse = []
            for j in range(SUB):
                inverse.append(lax.rsqrt(s[j][j]))
                for i in range(j + 1, SUB):
                    s[i][j] = s[i][j] * inverse[j]
                for k in range(j + 1, SUB):
                    for i in range(k, SUB):
                        s[i][k] = s[i][k] - s[i][j] * s[k][j]
            wide = lambda x: jnp.concatenate([x] * (WINDOW // LANES), axis=1)
            rows = []
            result = None
            for j in range(SUB):
                row = jnp.broadcast_to(groups[g][j:j + 1, :], (SUB, WINDOW))
                for m in range(j):
                    row = row - wide(s[j][m]) * rows[m]
                row = row * wide(inverse[j])
                rows.append(row)
                result = row if result is None else jnp.where(sublane == j, row, result)
            groups[g] = result
            for q in range(g + 1, PANEL // SUB):
                cols = []
                total = groups[q]
                for j in range(SUB):
                    col = columns[q - g][j]
                    for m in range(j):
                        col = col - cols[m] * s[j][m]
                    col = col * inverse[j]
                    cols.append(col)
                    total = total - wide(col) * rows[j]
                groups[q] = total
        panel = jnp.concatenate(groups, axis=0)
        work[top:top + PANEL, off:off + WINDOW] = panel
        rest = top + PANEL
        if rest < B:
            start = rest // LANES * LANES
            left = split(panel[:, start - off:B - off].T)
            update = product(left, split(panel), NN)[rest - start:]
            work[rest:, off:off + WINDOW] = work[rest:, off:off + WINDOW] - update


def finish(work, factor_ref, inverse_ref):
    row = lax.broadcasted_iota(jnp.int32, (B, B), 0)
    col = lax.broadcasted_iota(jnp.int32, (B, B), 1)
    factor_ref[...] = jnp.where(col >= row, work[:, :B], 0.0).T
    inverse_ref[...] = work[:, B:]


def start(work, block):
    row = lax.broadcasted_iota(jnp.int32, (B, B), 0)
    col = lax.broadcasted_iota(jnp.int32, (B, B), 1)
    work[:, :B] = block
    work[:, B:] = jnp.where(row == col, 1.0, 0.0).astype(F32)


def first_kernel(corner_ref, factor_ref, inverse_ref, work):
    start(work, corner_ref[0])
    eliminate(work)
    finish(work, factor_ref, inverse_ref)


def second_kernel(pattern, corner_ref, w_ref, lower_ref, factor_ref, inverse_ref, work):
    lower = product(split(corner_ref[1]), split(w_ref[...]), NT)
    lower = jnp.where(pattern[0, 1] == 1, lower, jnp.zeros_like(lower))
    lower_ref[...] = lower
    parts = split(lower)
    start(work, corner_ref[2] - product(parts, parts, NT))
    eliminate(work)
    finish(work, factor_ref, inverse_ref)


SQUARE = jax.ShapeDtypeStruct((B, B), F32)
ELIMINATION = pl.CostEstimate(flops=2 * B * B * B, bytes_accessed=24 << 20, transcendentals=0)


def factor_first(corner):
    return pl.pallas_call(
        first_kernel,
        out_shape=(SQUARE, SQUARE),
        scratch_shapes=[pltpu.VMEM((B, 2 * B), F32)],
        cost_estimate=ELIMINATION,
        name="factor_first",
    )(corner)


def factor_second(pattern, corner, w):
    vmem = pl.BlockSpec(memory_space=pltpu.VMEM)
    return pl.pallas_call(
        second_kernel,
        out_shape=(SQUARE, SQUARE, SQUARE),
        in_specs=[pl.BlockSpec(memory_space=pltpu.SMEM), vmem, vmem],
        scratch_shapes=[pltpu.VMEM((B, 2 * B), F32)],
        cost_estimate=ELIMINATION,
        name="factor_second",
    )(pattern, corner, w)


def panel_rows(first, second, flag0, flag1, w0, w1, lower):
    l0 = product(split(first), w0, NT)
    l0 = jnp.where(flag0, l0, jnp.zeros_like(l0))
    p0 = split(l0)
    l1 = product(split(second - product(p0, lower, NT)), w1, NT)
    l1 = jnp.where(flag1, l1, jnp.zeros_like(l1))
    return l0, l1, p0, split(l1)


def trailing_kernel(
    pattern, blocks_ref, rows_ref, cols_ref, w0_ref, w1_ref, lower_ref, g0_ref, g1_ref, out_ref,
    high0, low0, high1, low1, weights
):
    a = pl.program_id(0)
    count_c = high0.shape[0]
    prow, pcol = lax.axis_index("prow"), lax.axis_index("pcol")
    nprow, npcol = lax.axis_size("prow"), lax.axis_size("pcol")

    def flags(i):
        first = (pattern[0, i] == 1) & (i > 0)
        return first, ((pattern[1, i] == 1) | ((pattern[0, 1] == 1) & first)) & (i > 1)


    @pl.when(a == 0)
    def _():
        for n, ref in enumerate((w0_ref, w1_ref, lower_ref)):
            weights[2 * n], weights[2 * n + 1] = split(ref[...])
        for b in range(count_c):
            w0, w1, lower = ((weights[2 * n], weights[2 * n + 1]) for n in range(3))
            _, _, p0, p1 = panel_rows(
                cols_ref[0, b].T, cols_ref[1, b].T, *flags(pcol + npcol * b), w0, w1, lower
            )
            high0[b], low0[b] = p0
            high1[b], low1[b] = p1

    w0, w1, lower = ((weights[2 * n], weights[2 * n + 1]) for n in range(3))
    row = prow + nprow * a
    l0, l1, p0, p1 = panel_rows(rows_ref[0, 0], rows_ref[1, 0], *flags(row), w0, w1, lower)
    for b in range(count_c):
        col = pcol + npcol * b
        old = blocks_ref[0, b]

        @pl.when(col > row)
        def _():
            out_ref[0, b] = old

        @pl.when(col == 0)
        def _():
            out_ref[0, b] = jnp.where(row == 0, g0_ref[...], l0)

        @pl.when((col == 1) & (row >= 1))
        def _():
            out_ref[0, b] = jnp.where(row == 1, g1_ref[...], l1)

        @pl.when((col > 1) & (col <= row))
        def _():
            update = product(p0, (high0[b], low0[b]), NT) + product(p1, (high1[b], low1[b]), NT)
            out_ref[0, b] = old - update


def trailing(pattern, blocks, rows, cols, w0, w1, lower, g0, g1):
    count_r, count_c = blocks.shape[0], blocks.shape[1]
    whole = lambda shape: pl.BlockSpec(shape, lambda a: (0,) * len(shape))
    own = pl.BlockSpec((1, count_c, B, B), lambda a: (a, 0, 0, 0))
    return pl.pallas_call(
        trailing_kernel,
        grid=(count_r,),
        out_shape=jax.ShapeDtypeStruct(blocks.shape, F32),
        in_specs=[
            pl.BlockSpec(memory_space=pltpu.SMEM),
            own,
            pl.BlockSpec((2, 1, B, B), lambda a: (0, a, 0, 0)),
            whole((2, count_c, B, B)),
        ] + [whole((B, B))] * 5,
        out_specs=own,
        scratch_shapes=[pltpu.VMEM((count_c, B, B), BF16)] * 4 + [pltpu.VMEM((6, B, B), BF16)],
        name="trailing",
    )(pattern, blocks, rows, cols, w0, w1, lower, g0, g1)


CHIPS_X, CHIPS_Y, CHIPS_Z = 4, 8, 8
PIECES = 32
MESH = pl.DeviceIdType.MESH


def spread_kernel(
    blocks, rows, cols, corner, x_send, x_recv, z_send, z_recv, y_send, y_recv, core_send, core_recv, here
):
    prow, pcol = lax.axis_index("prow"), lax.axis_index("pcol")
    y, core = prow // 2, prow % 2
    z, x = pcol // CHIPS_X, pcol % CHIPS_X
    order = blocks.shape[2]
    piece = order * 4 // (2 * PIECES)

    def at_x(step):
        return {"pcol": z * CHIPS_X + (x + step + CHIPS_X) % CHIPS_X}

    def at_z(step):
        return {"pcol": (z + step + CHIPS_Z) % CHIPS_Z * CHIPS_X + x}

    def at_y(step):
        return {"prow": (y + step + CHIPS_Y) % CHIPS_Y * 2 + core}

    partner = {"prow": y * 2 + 1 - core}
    neighbours = [at(step) for at in (at_x, at_z, at_y) for step in (1, -1)] + [partner]
    barrier = pltpu.get_barrier_semaphore()
    for device in neighbours:
        pl.semaphore_signal(barrier, inc=1, device_id=device, device_id_type=MESH)
    pl.semaphore_wait(barrier, len(neighbours))

    def remote(ref, send, recv, device):
        return pltpu.make_async_remote_copy(
            src_ref=ref, dst_ref=ref, send_sem=send, recv_sem=recv, device_id=device, device_id_type=MESH
        )

    for n in (0, 1):
        @pl.when(pcol == n)
        def _():
            copy = pltpu.make_async_copy(blocks.at[:, 0], rows.at[n], here)
            copy.start()
            copy.wait()

    streams = []
    for n in (0, 1):
        for h in (0, 1):
            in_x = (x + CHIPS_X - n) % CHIPS_X if h == 0 else (n + CHIPS_X - x) % CHIPS_X
            in_z = z if h == 0 else (CHIPS_Z - z) % CHIPS_Z
            streams.append((n, h, in_x, in_z))
    deepest = streams[0][2] + streams[0][3]
    for _, _, in_x, in_z in streams[1:]:
        deepest = jnp.maximum(deepest, in_x + in_z)

    def row_copies(n, h, p):
        per = 2 * piece * (PIECES // 4) // 2
        first = pl.multiple_of(h * per + p % (PIECES // 4) * piece, piece)
        ref = rows.at[n, p // (PIECES // 4), pl.ds(first, piece)]
        k = (n * 2 + h) * PIECES + p
        step = 1 if h == 0 else -1
        return (
            remote(ref, x_send.at[k], x_recv.at[k], at_x(step)),
            remote(ref, z_send.at[k], z_recv.at[k], at_z(step)),
        )

    half_order = order // 2
    items = []
    for q in range(3):
        for k in (0, 1):
            part = pl.ds(k * half_order, half_order)
            source = min(q, 1)
            when = deepest + PIECES // 4 + 2 * q + k
            items.append((when, source, rows.at[q // 2, 0, part], corner.at[q, part]))
    for b in (0, 1):
        for k in (0, 1):
            part = pl.ds(k * half_order, half_order)
            for n in (0, 1):
                items.append((2 * (2 * b + k), n, blocks.at[0, b, part], cols.at[n, b, part]))
    far = CHIPS_Y // 2

    def item_copies(k, ref):
        return (
            remote(ref, y_send.at[2 * k], y_recv.at[k], at_y(1)),
            remote(ref, y_send.at[2 * k + 1], y_recv.at[k], at_y(-1)),
            remote(ref, core_send.at[k], core_recv.at[k], partner),
        )

    def place(source):
        ahead = (y + CHIPS_Y - source // 2) % CHIPS_Y
        up = ahead < far
        down = (ahead == 0) | (ahead > far + 1) if CHIPS_Y > 2 else ahead < 0
        return ahead, jnp.minimum(ahead, CHIPS_Y - ahead), up, down

    def step(t, carry):
        for n, h, in_x, in_z in streams:
            p = t - in_x - in_z

            @pl.when((p >= 0) & (p < PIECES))
            def _():
                along_x, along_z = row_copies(n, h, p)

                @pl.when((in_z == 0) & (in_x > 0))
                def _():
                    along_x.wait_recv()

                @pl.when(in_z > 0)
                def _():
                    along_z.wait_recv()

                @pl.when((in_z == 0) & (in_x < CHIPS_X - 1))
                def _():
                    along_x.start()

                @pl.when(in_z < CHIPS_Z - 1)
                def _():
                    along_z.start()

        for k, (when, source, origin, ref) in enumerate(items):
            ahead, depth, up, down = place(source)
            above, below, across = item_copies(k, ref)

            @pl.when((t == when + 2 * depth) & (core == source % 2))
            def _():
                @pl.when(ahead == 0)
                def _():
                    copy = pltpu.make_async_copy(origin, ref, here)
                    copy.start()
                    copy.wait()

                @pl.when(ahead > 0)
                def _():
                    above.wait_recv()

                @pl.when(up)
                def _():
                    above.start()

                @pl.when(down)
                def _():
                    below.start()

                across.start()

            @pl.when((t == when + 2 * depth + 2) & (core != source % 2))
            def _():
                across.wait_recv()

        return carry

    steps = CHIPS_X + CHIPS_Z - 2 + PIECES + 2 * far + 8
    lax.fori_loop(0, steps, step, 0)

    def drain(p, carry):
        for n, h, in_x, in_z in streams:
            along_x, along_z = row_copies(n, h, p)

            @pl.when((in_z == 0) & (in_x < CHIPS_X - 1))
            def _():
                along_x.wait_send()

            @pl.when(in_z < CHIPS_Z - 1)
            def _():
                along_z.wait_send()

        return carry

    lax.fori_loop(0, PIECES, drain, 0)
    for k, (_, source, _, ref) in enumerate(items):
        _, _, up, down = place(source)
        above, below, across = item_copies(k, ref)

        @pl.when(core == source % 2)
        def _():
            @pl.when(up)
            def _():
                above.wait_send()

            @pl.when(down)
            def _():
                below.wait_send()

            across.wait_send()


def spread(blocks):
    count, order = blocks.shape[0], blocks.shape[2]
    vmem = pl.BlockSpec(memory_space=pltpu.VMEM)
    shapes = ((2, count, order, order), (2, 2, order, order), (3, order, order))
    dma = pltpu.SemaphoreType.DMA
    return pl.pallas_call(
        spread_kernel,
        out_shape=tuple(jax.ShapeDtypeStruct(shape, F32) for shape in shapes),
        in_specs=[pl.BlockSpec(memory_space=pl.ANY)],
        out_specs=(vmem,) * 3,
        scratch_shapes=[dma((4 * PIECES,))] * 4 + [dma((28,)), dma((14,)), dma((14,)), dma((14,)), dma(())],
        compiler_params=pltpu.CompilerParams(collective_id=0, has_side_effects=True),
        name="spread",
    )(blocks)


def local(stiffness, pattern):
    blocks = stiffness.reshape(stiffness.shape[0], stiffness.shape[2], B, B)
    rows, cols, corner = spread(blocks)
    g0, w0 = factor_first(corner)
    lower, g1, w1 = factor_second(pattern, corner, w0)
    return trailing(pattern, blocks, rows, cols, w0, w1, lower, g0, g1).reshape(stiffness.shape)


def solution(mesh):
    placed = P(None, "prow", None, "pcol", None, None)
    return jax.shard_map(
        local, mesh=mesh, in_specs=(placed, P()), out_specs=placed, check_vma=False
    )
```

```python
import jax
import jax.numpy as jnp
from jax import lax
from jax.experimental import pallas as pl
from jax.experimental.pallas import tpu as pltpu
from jax.sharding import PartitionSpec as P

B = 256
PANEL = 32
SUB = 8
LANES = 128
WINDOW = 3 * LANES
F32 = jnp.float32
BF16 = jnp.bfloat16


def split(x):
    high = x.astype(BF16)
    return high, (x - high.astype(F32)).astype(BF16)


def product(a, b, dims):
    dot = lambda x, y: lax.dot_general(x, y, (dims, ((), ())), preferred_element_type=F32)
    return dot(a[0], b[0]) + (dot(a[0], b[1]) + dot(a[1], b[0]))


NT = ((1,), (1,))
NN = ((1,), (0,))


def eliminate(work):
    spread = lambda x: jnp.broadcast_to(x, (SUB, LANES))
    sublane = lax.broadcasted_iota(jnp.int32, (SUB, WINDOW), 0)
    for top in range(0, B, PANEL):
        off = top // LANES * LANES
        groups = [work[top + SUB * q:top + SUB * (q + 1), off:off + WINDOW] for q in range(PANEL // SUB)]
        for g in range(PANEL // SUB):
            lane = top + SUB * g - off
            columns = [
                [spread(groups[q][:, lane + j:lane + j + 1]) for j in range(SUB)]
                for q in range(g, PANEL // SUB)
            ]
            s = [[spread(columns[0][j][i:i + 1, :]) for j in range(i + 1)] for i in range(SUB)]
            inverse = []
            for j in range(SUB):
                inverse.append(lax.rsqrt(s[j][j]))
                for i in range(j + 1, SUB):
                    s[i][j] = s[i][j] * inverse[j]
                for k in range(j + 1, SUB):
                    for i in range(k, SUB):
                        s[i][k] = s[i][k] - s[i][j] * s[k][j]
            wide = lambda x: jnp.concatenate([x] * (WINDOW // LANES), axis=1)
            rows = []
            result = None
            for j in range(SUB):
                row = jnp.broadcast_to(groups[g][j:j + 1, :], (SUB, WINDOW))
                for m in range(j):
                    row = row - wide(s[j][m]) * rows[m]
                row = row * wide(inverse[j])
                rows.append(row)
                result = row if result is None else jnp.where(sublane == j, row, result)
            groups[g] = result
            for q in range(g + 1, PANEL // SUB):
                cols = []
                total = groups[q]
                for j in range(SUB):
                    col = columns[q - g][j]
                    for m in range(j):
                        col = col - cols[m] * s[j][m]
                    col = col * inverse[j]
                    cols.append(col)
                    total = total - wide(col) * rows[j]
                groups[q] = total
        panel = jnp.concatenate(groups, axis=0)
        work[top:top + PANEL, off:off + WINDOW] = panel
        rest = top + PANEL
        if rest < B:
            start = rest // LANES * LANES
            left = split(panel[:, start - off:B - off].T)
            update = product(left, split(panel), NN)[rest - start:]
            work[rest:, off:off + WINDOW] = work[rest:, off:off + WINDOW] - update


def finish(work, factor_ref, inverse_ref):
    row = lax.broadcasted_iota(jnp.int32, (B, B), 0)
    col = lax.broadcasted_iota(jnp.int32, (B, B), 1)
    factor_ref[...] = jnp.where(col >= row, work[:, :B], 0.0).T
    inverse_ref[...] = work[:, B:]


def start(work, block):
    row = lax.broadcasted_iota(jnp.int32, (B, B), 0)
    col = lax.broadcasted_iota(jnp.int32, (B, B), 1)
    work[:, :B] = block
    work[:, B:] = jnp.where(row == col, 1.0, 0.0).astype(F32)


def first_kernel(corner_ref, factor_ref, inverse_ref, work):
    start(work, corner_ref[0])
    eliminate(work)
    finish(work, factor_ref, inverse_ref)


def second_kernel(pattern, corner_ref, w_ref, lower_ref, factor_ref, inverse_ref, work):
    lower = product(split(corner_ref[1]), split(w_ref[...]), NT)
    lower = jnp.where(pattern[0, 1] == 1, lower, jnp.zeros_like(lower))
    lower_ref[...] = lower
    parts = split(lower)
    start(work, corner_ref[2] - product(parts, parts, NT))
    eliminate(work)
    finish(work, factor_ref, inverse_ref)


SQUARE = jax.ShapeDtypeStruct((B, B), F32)
ELIMINATION = pl.CostEstimate(flops=2 * B * B * B, bytes_accessed=24 << 20, transcendentals=0)


def factor_first(corner):
    return pl.pallas_call(
        first_kernel,
        out_shape=(SQUARE, SQUARE),
        scratch_shapes=[pltpu.VMEM((B, 2 * B), F32)],
        cost_estimate=ELIMINATION,
        name="factor_first",
    )(corner)


def factor_second(pattern, corner, w):
    vmem = pl.BlockSpec(memory_space=pltpu.VMEM)
    return pl.pallas_call(
        second_kernel,
        out_shape=(SQUARE, SQUARE, SQUARE),
        in_specs=[pl.BlockSpec(memory_space=pltpu.SMEM), vmem, vmem],
        scratch_shapes=[pltpu.VMEM((B, 2 * B), F32)],
        cost_estimate=ELIMINATION,
        name="factor_second",
    )(pattern, corner, w)


def panel_rows(first, second, flag0, flag1, w0, w1, lower):
    l0 = product(split(first), w0, NT)
    l0 = jnp.where(flag0, l0, jnp.zeros_like(l0))
    p0 = split(l0)
    l1 = product(split(second - product(p0, lower, NT)), w1, NT)
    l1 = jnp.where(flag1, l1, jnp.zeros_like(l1))
    return l0, l1, p0, split(l1)


def trailing_kernel(
    pattern, blocks_ref, rows_ref, cols_ref, w0_ref, w1_ref, lower_ref, g0_ref, g1_ref, out_ref,
    high0, low0, high1, low1, weights
):
    a = pl.program_id(0)
    count_c = high0.shape[0]
    prow, pcol = lax.axis_index("prow"), lax.axis_index("pcol")
    nprow, npcol = lax.axis_size("prow"), lax.axis_size("pcol")

    def flags(i):
        first = (pattern[0, i] == 1) & (i > 0)
        return first, ((pattern[1, i] == 1) | ((pattern[0, 1] == 1) & first)) & (i > 1)


    @pl.when(a == 0)
    def _():
        for n, ref in enumerate((w0_ref, w1_ref, lower_ref)):
            weights[2 * n], weights[2 * n + 1] = split(ref[...])
        for b in range(count_c):
            w0, w1, lower = ((weights[2 * n], weights[2 * n + 1]) for n in range(3))
            _, _, p0, p1 = panel_rows(
                cols_ref[0, b].T, cols_ref[1, b].T, *flags(pcol + npcol * b), w0, w1, lower
            )
            high0[b], low0[b] = p0
            high1[b], low1[b] = p1

    w0, w1, lower = ((weights[2 * n], weights[2 * n + 1]) for n in range(3))
    row = prow + nprow * a
    l0, l1, p0, p1 = panel_rows(rows_ref[0, 0], rows_ref[1, 0], *flags(row), w0, w1, lower)
    for b in range(count_c):
        col = pcol + npcol * b
        old = blocks_ref[0, b]

        @pl.when(col > row)
        def _():
            out_ref[0, b] = old

        @pl.when(col == 0)
        def _():
            out_ref[0, b] = jnp.where(row == 0, g0_ref[...], l0)

        @pl.when((col == 1) & (row >= 1))
        def _():
            out_ref[0, b] = jnp.where(row == 1, g1_ref[...], l1)

        @pl.when((col > 1) & (col <= row))
        def _():
            update = product(p0, (high0[b], low0[b]), NT) + product(p1, (high1[b], low1[b]), NT)
            out_ref[0, b] = old - update


def trailing(pattern, blocks, rows, cols, w0, w1, lower, g0, g1):
    count_r, count_c = blocks.shape[0], blocks.shape[1]
    whole = lambda shape: pl.BlockSpec(shape, lambda a: (0,) * len(shape))
    own = pl.BlockSpec((1, count_c, B, B), lambda a: (a, 0, 0, 0))
    return pl.pallas_call(
        trailing_kernel,
        grid=(count_r,),
        out_shape=jax.ShapeDtypeStruct(blocks.shape, F32),
        in_specs=[
            pl.BlockSpec(memory_space=pltpu.SMEM),
            own,
            pl.BlockSpec((2, 1, B, B), lambda a: (0, a, 0, 0)),
            whole((2, count_c, B, B)),
        ] + [whole((B, B))] * 5,
        out_specs=own,
        scratch_shapes=[pltpu.VMEM((count_c, B, B), BF16)] * 4 + [pltpu.VMEM((6, B, B), BF16)],
        name="trailing",
    )(pattern, blocks, rows, cols, w0, w1, lower, g0, g1)


CHIPS_X, CHIPS_Y, CHIPS_Z = 4, 8, 8
PIECES = 16
HOP = 2
MESH = pl.DeviceIdType.MESH


def spread_kernel(
    blocks, rows, cols, corner, x_send, x_recv, z_send, z_recv, y_send, y_recv, core_send, core_recv, here
):
    prow, pcol = lax.axis_index("prow"), lax.axis_index("pcol")
    y, core = prow // 2, prow % 2
    z, x = pcol // CHIPS_X, pcol % CHIPS_X
    order = blocks.shape[2]
    piece = order * 4 // (2 * PIECES)

    def at_x(step):
        return {"pcol": z * CHIPS_X + (x + step + CHIPS_X) % CHIPS_X}

    def at_z(step):
        return {"pcol": (z + step + CHIPS_Z) % CHIPS_Z * CHIPS_X + x}

    def at_y(step):
        return {"prow": (y + step + CHIPS_Y) % CHIPS_Y * 2 + core}

    partner = {"prow": y * 2 + 1 - core}
    sides_x, sides_y, sides_z = ({step: at(step) for step in (1, -1)} for at in (at_x, at_y, at_z))
    neighbours = [sides[step] for sides in (sides_x, sides_z, sides_y) for step in (1, -1)] + [partner]
    barrier = pltpu.get_barrier_semaphore()
    for device in neighbours:
        pl.semaphore_signal(barrier, inc=1, device_id=device, device_id_type=MESH)
    pl.semaphore_wait(barrier, len(neighbours))

    def remote(ref, send, recv, device):
        return pltpu.make_async_remote_copy(
            src_ref=ref, dst_ref=ref, send_sem=send, recv_sem=recv, device_id=device, device_id_type=MESH
        )

    for n in (0, 1):
        @pl.when(pcol == n)
        def _():
            copy = pltpu.make_async_copy(blocks.at[:, 0], rows.at[n], here)
            copy.start()
            copy.wait()

    streams = []
    for n in (0, 1):
        for h in (0, 1):
            in_x = (x + CHIPS_X - n) % CHIPS_X if h == 0 else (n + CHIPS_X - x) % CHIPS_X
            in_z = z if h == 0 else (CHIPS_Z - z) % CHIPS_Z
            streams.append((n, h, in_x, in_z))
    deepest = streams[0][2] + streams[0][3]
    for _, _, in_x, in_z in streams[1:]:
        deepest = jnp.maximum(deepest, in_x + in_z)

    def row_copies(n, h, p):
        per = 2 * piece * (PIECES // 4) // 2
        first = pl.multiple_of(h * per + p % (PIECES // 4) * piece, piece)
        ref = rows.at[n, p // (PIECES // 4), pl.ds(first, piece)]
        k = (n * 2 + h) * PIECES + p
        step = 1 if h == 0 else -1
        return (
            remote(ref, x_send.at[k], x_recv.at[k], sides_x[step]),
            remote(ref, z_send.at[k], z_recv.at[k], sides_z[step]),
        )

    half_order = order // 2
    items = []
    for q in range(3):
        for k in (0, 1):
            part = pl.ds(k * half_order, half_order)
            source = min(q, 1)
            when = HOP * deepest + PIECES // 4 + q
            items.append((when, source, rows.at[q // 2, 0, part], corner.at[q, part]))
    for b in (0, 1):
        for k in (0, 1):
            part = pl.ds(k * half_order, half_order)
            for n in (0, 1):
                items.append((2 * (2 * b + k), n, blocks.at[0, b, part], cols.at[n, b, part]))
    far = CHIPS_Y // 2

    def item_copies(k, ref):
        return (
            remote(ref, y_send.at[2 * k], y_recv.at[k], sides_y[1]),
            remote(ref, y_send.at[2 * k + 1], y_recv.at[k], sides_y[-1]),
            remote(ref, core_send.at[k], core_recv.at[k], partner),
        )


    down = (y == 0) | (y > far + 1) if CHIPS_Y > 2 else y < 0
    placed = y, jnp.minimum(y, CHIPS_Y - y), y < far, down

    def step(t, carry):
        for n, h, in_x, in_z in streams:
            p = t - HOP * (in_x + in_z)

            @pl.when((p >= 0) & (p < PIECES))
            def _():
                along_x, along_z = row_copies(n, h, p)

                @pl.when((in_z == 0) & (in_x > 0))
                def _():
                    along_x.wait_recv()

                @pl.when(in_z > 0)
                def _():
                    along_z.wait_recv()

                @pl.when((in_z == 0) & (in_x < CHIPS_X - 1))
                def _():
                    along_x.start()

                @pl.when(in_z < CHIPS_Z - 1)
                def _():
                    along_z.start()

        for k, (when, source, origin, ref) in enumerate(items):
            ahead, depth, up, down = placed
            above, below, across = item_copies(k, ref)

            @pl.when((t == when + 2 * depth) & (core == source % 2))
            def _():
                @pl.when(ahead == 0)
                def _():
                    copy = pltpu.make_async_copy(origin, ref, here)
                    copy.start()
                    copy.wait()

                @pl.when(ahead > 0)
                def _():
                    above.wait_recv()

                @pl.when(up)
                def _():
                    above.start()

                @pl.when(down)
                def _():
                    below.start()

                across.start()

            @pl.when((t == when + 2 * depth + 2) & (core != source % 2))
            def _():
                across.wait_recv()

        return carry

    steps = HOP * (CHIPS_X + CHIPS_Z - 2) + max(PIECES, PIECES // 4 + 2 * far + 4) + 2
    lax.fori_loop(0, steps, step, 0)

    def drain(p, carry):
        for n, h, in_x, in_z in streams:
            along_x, along_z = row_copies(n, h, p)

            @pl.when((in_z == 0) & (in_x < CHIPS_X - 1))
            def _():
                along_x.wait_send()

            @pl.when(in_z < CHIPS_Z - 1)
            def _():
                along_z.wait_send()

        return carry

    lax.fori_loop(0, PIECES, drain, 0)
    for k, (_, source, _, ref) in enumerate(items):
        _, _, up, down = placed
        above, below, across = item_copies(k, ref)

        @pl.when(core == source % 2)
        def _():
            @pl.when(up)
            def _():
                above.wait_send()

            @pl.when(down)
            def _():
                below.wait_send()

            across.wait_send()


def spread(blocks):
    count, order = blocks.shape[0], blocks.shape[2]
    vmem = pl.BlockSpec(memory_space=pltpu.VMEM)
    shapes = ((2, count, order, order), (2, 2, order, order), (3, order, order))
    dma = pltpu.SemaphoreType.DMA
    return pl.pallas_call(
        spread_kernel,
        out_shape=tuple(jax.ShapeDtypeStruct(shape, F32) for shape in shapes),
        in_specs=[pl.BlockSpec(memory_space=pl.ANY)],
        out_specs=(vmem,) * 3,
        scratch_shapes=[dma((4 * PIECES,))] * 4 + [dma((28,)), dma((14,)), dma((14,)), dma((14,)), dma(())],
        compiler_params=pltpu.CompilerParams(collective_id=0, has_side_effects=True),
        name="spread",
    )(blocks)


def local(stiffness, pattern):
    blocks = stiffness.reshape(stiffness.shape[0], stiffness.shape[2], B, B)
    rows, cols, corner = spread(blocks)
    g0, w0 = factor_first(corner)
    lower, g1, w1 = factor_second(pattern, corner, w0)
    return trailing(pattern, blocks, rows, cols, w0, w1, lower, g0, g1).reshape(stiffness.shape)


def solution(mesh):
    placed = P(None, "prow", None, "pcol", None, None)
    return jax.shard_map(
        local, mesh=mesh, in_specs=(placed, P()), out_specs=placed, check_vma=False
    )
```

```python
import jax
import jax.numpy as jnp
from jax import lax
from jax.experimental import pallas as pl
from jax.experimental.pallas import tpu as pltpu
from jax.sharding import PartitionSpec as P

B = 256
PANEL = 32
SUB = 8
LANES = 128
WINDOW = 3 * LANES
F32 = jnp.float32
BF16 = jnp.bfloat16


def split(x):
    high = x.astype(BF16)
    return high, (x - high.astype(F32)).astype(BF16)


def product(a, b, dims):
    dot = lambda x, y: lax.dot_general(x, y, (dims, ((), ())), preferred_element_type=F32)
    return dot(a[0], b[0]) + (dot(a[0], b[1]) + dot(a[1], b[0]))


NT = ((1,), (1,))
NN = ((1,), (0,))


def eliminate(work):
    spread = lambda x: jnp.broadcast_to(x, (SUB, LANES))
    sublane = lax.broadcasted_iota(jnp.int32, (SUB, WINDOW), 0)
    for top in range(0, B, PANEL):
        off = top // LANES * LANES
        groups = [work[top + SUB * q:top + SUB * (q + 1), off:off + WINDOW] for q in range(PANEL // SUB)]
        for g in range(PANEL // SUB):
            lane = top + SUB * g - off
            columns = [
                [spread(groups[q][:, lane + j:lane + j + 1]) for j in range(SUB)]
                for q in range(g, PANEL // SUB)
            ]
            s = [[spread(columns[0][j][i:i + 1, :]) for j in range(i + 1)] for i in range(SUB)]
            inverse = []
            for j in range(SUB):
                inverse.append(lax.rsqrt(s[j][j]))
                for i in range(j + 1, SUB):
                    s[i][j] = s[i][j] * inverse[j]
                for k in range(j + 1, SUB):
                    for i in range(k, SUB):
                        s[i][k] = s[i][k] - s[i][j] * s[k][j]
            wide = lambda x: jnp.concatenate([x] * (WINDOW // LANES), axis=1)
            rows = []
            result = None
            for j in range(SUB):
                row = jnp.broadcast_to(groups[g][j:j + 1, :], (SUB, WINDOW))
                for m in range(j):
                    row = row - wide(s[j][m]) * rows[m]
                row = row * wide(inverse[j])
                rows.append(row)
                result = row if result is None else jnp.where(sublane == j, row, result)
            groups[g] = result
            for q in range(g + 1, PANEL // SUB):
                cols = []
                total = groups[q]
                for j in range(SUB):
                    col = columns[q - g][j]
                    for m in range(j):
                        col = col - cols[m] * s[j][m]
                    col = col * inverse[j]
                    cols.append(col)
                    total = total - wide(col) * rows[j]
                groups[q] = total
        panel = jnp.concatenate(groups, axis=0)
        work[top:top + PANEL, off:off + WINDOW] = panel
        rest = top + PANEL
        if rest < B:
            start = rest // LANES * LANES
            left = split(panel[:, start - off:B - off].T)
            update = product(left, split(panel), NN)[rest - start:]
            work[rest:, off:off + WINDOW] = work[rest:, off:off + WINDOW] - update


def finish(work, factor_ref, inverse_ref):
    row = lax.broadcasted_iota(jnp.int32, (B, B), 0)
    col = lax.broadcasted_iota(jnp.int32, (B, B), 1)
    factor_ref[...] = jnp.where(col >= row, work[:, :B], 0.0).T
    inverse_ref[...] = work[:, B:]


def start(work, block):
    row = lax.broadcasted_iota(jnp.int32, (B, B), 0)
    col = lax.broadcasted_iota(jnp.int32, (B, B), 1)
    work[:, :B] = block
    work[:, B:] = jnp.where(row == col, 1.0, 0.0).astype(F32)


def first_kernel(corner_ref, factor_ref, inverse_ref, work):
    start(work, corner_ref[0])
    eliminate(work)
    finish(work, factor_ref, inverse_ref)


def second_kernel(pattern, corner_ref, w_ref, lower_ref, factor_ref, inverse_ref, work):
    lower = product(split(corner_ref[1]), split(w_ref[...]), NT)
    lower = jnp.where(pattern[0, 1] == 1, lower, jnp.zeros_like(lower))
    lower_ref[...] = lower
    parts = split(lower)
    start(work, corner_ref[2] - product(parts, parts, NT))
    eliminate(work)
    finish(work, factor_ref, inverse_ref)


SQUARE = jax.ShapeDtypeStruct((B, B), F32)
ELIMINATION = pl.CostEstimate(flops=2 * B * B * B, bytes_accessed=24 << 20, transcendentals=0)


def factor_first(corner):
    return pl.pallas_call(
        first_kernel,
        out_shape=(SQUARE, SQUARE),
        scratch_shapes=[pltpu.VMEM((B, 2 * B), F32)],
        cost_estimate=ELIMINATION,
        name="factor_first",
    )(corner)


def factor_second(pattern, corner, w):
    vmem = pl.BlockSpec(memory_space=pltpu.VMEM)
    return pl.pallas_call(
        second_kernel,
        out_shape=(SQUARE, SQUARE, SQUARE),
        in_specs=[pl.BlockSpec(memory_space=pltpu.SMEM), vmem, vmem],
        scratch_shapes=[pltpu.VMEM((B, 2 * B), F32)],
        cost_estimate=ELIMINATION,
        name="factor_second",
    )(pattern, corner, w)


def panel_rows(first, second, flag0, flag1, w0, w1, lower):
    l0 = product(split(first), w0, NT)
    l0 = jnp.where(flag0, l0, jnp.zeros_like(l0))
    p0 = split(l0)
    l1 = product(split(second - product(p0, lower, NT)), w1, NT)
    l1 = jnp.where(flag1, l1, jnp.zeros_like(l1))
    return l0, l1, p0, split(l1)


def trailing_kernel(
    pattern, blocks_ref, rows_ref, cols_ref, w0_ref, w1_ref, lower_ref, g0_ref, g1_ref, out_ref,
    high0, low0, high1, low1, weights
):
    a = pl.program_id(0)
    count_c = high0.shape[0]
    prow, pcol = lax.axis_index("prow"), lax.axis_index("pcol")
    nprow, npcol = lax.axis_size("prow"), lax.axis_size("pcol")

    def flags(i):
        first = (pattern[0, i] == 1) & (i > 0)
        return first, ((pattern[1, i] == 1) | ((pattern[0, 1] == 1) & first)) & (i > 1)


    @pl.when(a == 0)
    def _():
        for n, ref in enumerate((w0_ref, w1_ref, lower_ref)):
            weights[2 * n], weights[2 * n + 1] = split(ref[...])
        for b in range(count_c):
            w0, w1, lower = ((weights[2 * n], weights[2 * n + 1]) for n in range(3))
            _, _, p0, p1 = panel_rows(
                cols_ref[0, b].T, cols_ref[1, b].T, *flags(pcol + npcol * b), w0, w1, lower
            )
            high0[b], low0[b] = p0
            high1[b], low1[b] = p1

    w0, w1, lower = ((weights[2 * n], weights[2 * n + 1]) for n in range(3))
    row = prow + nprow * a
    l0, l1, p0, p1 = panel_rows(rows_ref[0, 0], rows_ref[1, 0], *flags(row), w0, w1, lower)
    for b in range(count_c):
        col = pcol + npcol * b
        old = blocks_ref[0, b]

        @pl.when(col > row)
        def _():
            out_ref[0, b] = old

        @pl.when(col == 0)
        def _():
            out_ref[0, b] = jnp.where(row == 0, g0_ref[...], l0)

        @pl.when((col == 1) & (row >= 1))
        def _():
            out_ref[0, b] = jnp.where(row == 1, g1_ref[...], l1)

        @pl.when((col > 1) & (col <= row))
        def _():
            update = product(p0, (high0[b], low0[b]), NT) + product(p1, (high1[b], low1[b]), NT)
            out_ref[0, b] = old - update


def trailing(pattern, blocks, rows, cols, w0, w1, lower, g0, g1):
    count_r, count_c = blocks.shape[0], blocks.shape[1]
    whole = lambda shape: pl.BlockSpec(shape, lambda a: (0,) * len(shape))
    own = pl.BlockSpec((1, count_c, B, B), lambda a: (a, 0, 0, 0))
    return pl.pallas_call(
        trailing_kernel,
        grid=(count_r,),
        out_shape=jax.ShapeDtypeStruct(blocks.shape, F32),
        in_specs=[
            pl.BlockSpec(memory_space=pltpu.SMEM),
            own,
            pl.BlockSpec((2, 1, B, B), lambda a: (0, a, 0, 0)),
            whole((2, count_c, B, B)),
        ] + [whole((B, B))] * 5,
        out_specs=own,
        scratch_shapes=[pltpu.VMEM((count_c, B, B), BF16)] * 4 + [pltpu.VMEM((6, B, B), BF16)],
        name="trailing",
    )(pattern, blocks, rows, cols, w0, w1, lower, g0, g1)


CHIPS_X, CHIPS_Y, CHIPS_Z = 4, 8, 8
PIECES = 32
HOP = 3
HOP_Y = 4
MESH = pl.DeviceIdType.MESH


def spread_kernel(
    blocks, rows, cols, corner, x_send, x_recv, z_send, z_recv, y_send, y_recv, core_send, core_recv, here
):
    prow, pcol = lax.axis_index("prow"), lax.axis_index("pcol")
    y, core = prow // 2, prow % 2
    z, x = pcol // CHIPS_X, pcol % CHIPS_X
    order = blocks.shape[2]
    piece = order * 4 // (2 * PIECES)

    def at_x(step):
        return {"pcol": z * CHIPS_X + (x + step + CHIPS_X) % CHIPS_X}

    def at_z(step):
        return {"pcol": (z + step + CHIPS_Z) % CHIPS_Z * CHIPS_X + x}

    def at_y(step):
        return {"prow": (y + step + CHIPS_Y) % CHIPS_Y * 2 + core}

    partner = {"prow": y * 2 + 1 - core}
    sides_x, sides_y, sides_z = ({step: at(step) for step in (1, -1)} for at in (at_x, at_y, at_z))
    neighbours = [sides[step] for sides in (sides_x, sides_z, sides_y) for step in (1, -1)] + [partner]
    barrier = pltpu.get_barrier_semaphore()
    for device in neighbours:
        pl.semaphore_signal(barrier, inc=1, device_id=device, device_id_type=MESH)
    pl.semaphore_wait(barrier, len(neighbours))

    def remote(ref, send, recv, device):
        return pltpu.make_async_remote_copy(
            src_ref=ref, dst_ref=ref, send_sem=send, recv_sem=recv, device_id=device, device_id_type=MESH
        )

    for n in (0, 1):
        @pl.when(pcol == n)
        def _():
            copy = pltpu.make_async_copy(blocks.at[:, 0], rows.at[n], here)
            copy.start()
            copy.wait()

    streams = []
    for n in (0, 1):
        for h in (0, 1):
            in_x = (x + CHIPS_X - n) % CHIPS_X if h == 0 else (n + CHIPS_X - x) % CHIPS_X
            in_z = z if h == 0 else (CHIPS_Z - z) % CHIPS_Z
            streams.append((n, h, in_x, in_z))
    deepest = streams[0][2] + streams[0][3]
    for _, _, in_x, in_z in streams[1:]:
        deepest = jnp.maximum(deepest, in_x + in_z)

    def row_copies(n, h, p):
        per = 2 * piece * (PIECES // 4) // 2
        first = pl.multiple_of(h * per + p % (PIECES // 4) * piece, piece)
        ref = rows.at[n, p // (PIECES // 4), pl.ds(first, piece)]
        k = (n * 2 + h) * PIECES + p
        step = 1 if h == 0 else -1
        return (
            remote(ref, x_send.at[k], x_recv.at[k], sides_x[step]),
            remote(ref, z_send.at[k], z_recv.at[k], sides_z[step]),
        )

    half_order = order // 2
    items = []
    for q in range(3):
        for k in (0, 1):
            part = pl.ds(k * half_order, half_order)
            source = min(q, 1)
            when = HOP * deepest + PIECES // 4 + q
            items.append((when, source, rows.at[q // 2, 0, part], corner.at[q, part]))
    for b in (0, 1):
        for k in (0, 1):
            part = pl.ds(k * half_order, half_order)
            for n in (0, 1):
                items.append((HOP_Y * (2 * b + k), n, blocks.at[0, b, part], cols.at[n, b, part]))
    far = CHIPS_Y // 2

    def item_copies(k, ref):
        return (
            remote(ref, y_send.at[2 * k], y_recv.at[k], sides_y[1]),
            remote(ref, y_send.at[2 * k + 1], y_recv.at[k], sides_y[-1]),
            remote(ref, core_send.at[k], core_recv.at[k], partner),
        )


    down = (y == 0) | (y > far + 1) if CHIPS_Y > 2 else y < 0
    placed = y, jnp.minimum(y, CHIPS_Y - y), y < far, down

    def step(t, carry):
        for n, h, in_x, in_z in streams:
            p = t - HOP * (in_x + in_z)

            @pl.when((p >= 0) & (p < PIECES))
            def _():
                along_x, along_z = row_copies(n, h, p)

                @pl.when((in_z == 0) & (in_x > 0))
                def _():
                    along_x.wait_recv()

                @pl.when(in_z > 0)
                def _():
                    along_z.wait_recv()

                @pl.when((in_z == 0) & (in_x < CHIPS_X - 1))
                def _():
                    along_x.start()

                @pl.when(in_z < CHIPS_Z - 1)
                def _():
                    along_z.start()

        for k, (when, source, origin, ref) in enumerate(items):
            ahead, depth, up, down = placed
            above, below, across = item_copies(k, ref)

            @pl.when((t == when + HOP_Y * depth) & (core == source % 2))
            def _():
                @pl.when(ahead == 0)
                def _():
                    copy = pltpu.make_async_copy(origin, ref, here)
                    copy.start()
                    copy.wait()

                @pl.when(ahead > 0)
                def _():
                    above.wait_recv()

                @pl.when(up)
                def _():
                    above.start()

                @pl.when(down)
                def _():
                    below.start()

                across.start()

            @pl.when((t == when + HOP_Y * (depth + 1)) & (core != source % 2))
            def _():
                across.wait_recv()

        return carry

    steps = HOP * (CHIPS_X + CHIPS_Z - 2) + max(PIECES, PIECES // 4 + 2 + HOP_Y * (far + 1)) + 2
    lax.fori_loop(0, steps, step, 0)

    def drain(p, carry):
        for n, h, in_x, in_z in streams:
            along_x, along_z = row_copies(n, h, p)

            @pl.when((in_z == 0) & (in_x < CHIPS_X - 1))
            def _():
                along_x.wait_send()

            @pl.when(in_z < CHIPS_Z - 1)
            def _():
                along_z.wait_send()

        return carry

    lax.fori_loop(0, PIECES, drain, 0)
    for k, (_, source, _, ref) in enumerate(items):
        _, _, up, down = placed
        above, below, across = item_copies(k, ref)

        @pl.when(core == source % 2)
        def _():
            @pl.when(up)
            def _():
                above.wait_send()

            @pl.when(down)
            def _():
                below.wait_send()

            across.wait_send()


def spread(blocks):
    count, order = blocks.shape[0], blocks.shape[2]
    vmem = pl.BlockSpec(memory_space=pltpu.VMEM)
    shapes = ((2, count, order, order), (2, 2, order, order), (3, order, order))
    dma = pltpu.SemaphoreType.DMA
    return pl.pallas_call(
        spread_kernel,
        out_shape=tuple(jax.ShapeDtypeStruct(shape, F32) for shape in shapes),
        in_specs=[pl.BlockSpec(memory_space=pl.ANY)],
        out_specs=(vmem,) * 3,
        scratch_shapes=[dma((4 * PIECES,))] * 4 + [dma((28,)), dma((14,)), dma((14,)), dma((14,)), dma(())],
        compiler_params=pltpu.CompilerParams(collective_id=0, has_side_effects=True),
        name="spread",
    )(blocks)


def local(stiffness, pattern):
    blocks = stiffness.reshape(stiffness.shape[0], stiffness.shape[2], B, B)
    rows, cols, corner = spread(blocks)
    g0, w0 = factor_first(corner)
    lower, g1, w1 = factor_second(pattern, corner, w0)
    return trailing(pattern, blocks, rows, cols, w0, w1, lower, g0, g1).reshape(stiffness.shape)


def solution(mesh):
    placed = P(None, "prow", None, "pcol", None, None)
    return jax.shard_map(
        local, mesh=mesh, in_specs=(placed, P()), out_specs=placed, check_vma=False
    )
```
